128 devices in a mesh: dp: 4 (over y), seq: 32 (over z, x, core).
Axes of the slice: x: 4, y: 4, z: 4, core: 2. Of those that a mesh axis runs over, the one named last changes fastest.
Arguments:
- queries: bfloat16 [4, 8192, 1024], P('dp', 'seq'), may hold values from -7.5 to 7.5
- keys: bfloat16 [4, 8192, 1024], P('dp', 'seq'), may hold values from -7.5 to 7.5
- values: bfloat16 [4, 8192, 1024], P('dp', 'seq'), may hold values from -7.5 to 7.5
- grad_out: bfloat16 [4, 8192, 1024], P('dp', 'seq'), may hold values from -3 to 3
- w_out: bfloat16 [1024, 1024], replicated, may hold values from -0.1875 to 0.1875
Outputs:
- mixed: bfloat16 [4, 8192, 1024], P('dp', 'seq')
- grad_queries: bfloat16 [4, 8192, 1024], P('dp', 'seq')
- grad_keys: bfloat16 [4, 8192, 1024], P('dp', 'seq')
- grad_values: bfloat16 [4, 8192, 1024], P('dp', 'seq')
- grad_w_out: float32 [1024, 1024], P(('dp', 'seq'))
The draws below stay inside these ranges and needn't reach their ends.
All inputs are finite; a program needn't handle non-finite values.
Results may differ from the reference program's by a relative error of at most 0.03.
Values may be sent and summed in bfloat16 or wider, within the bound.
A program may use at most 128 MiB of HBM per device.

```python
import math
import jax
import jax.numpy as jnp
from jax import lax

HEADS = 8
HEAD_DIM = 128
D = 1024
BLOCK = 128
TOK_DEV = 256
LEVELS = 6
SEQ_LEN = 8192
SEQS = 4


def segment_field(key, gain, region_gain):
    segment = BLOCK // 2
    means = jax.random.normal(jax.random.fold_in(key, 1), (SEQS, SEQ_LEN // segment, D), jnp.float32)
    regions = jax.random.normal(jax.random.fold_in(key, 3), (SEQS, SEQ_LEN // TOK_DEV, D), jnp.float32)
    noise = jax.random.normal(jax.random.fold_in(key, 2), (SEQS, SEQ_LEN, D), jnp.float32)
    field = gain * (jnp.repeat(means, segment, axis=1) + noise) + region_gain * jnp.repeat(regions, TOK_DEV, axis=1)
    return jnp.clip(field, -7.5, 7.5)


def drawn_pair(key):
    query_field = segment_field(jax.random.fold_in(key, 101), 0.6, 0.0)
    key_field = segment_field(jax.random.fold_in(key, 202), 0.6, 0.0)
    return (query_field, key_field)


def draw_queries(key, part):
    return drawn_pair(key)[0].astype(jnp.bfloat16)


def draw_keys(key, part):
    return drawn_pair(key)[1].astype(jnp.bfloat16)


def draw_values(key, part):
    return segment_field(jax.random.fold_in(key, 404), 1.0, 1.5).astype(jnp.bfloat16)


def block_levels(key, extent, split, low, largest):
    level = 1.0
    for axis_at, shards_of in split:
        heights = jax.random.uniform(jax.random.fold_in(jax.random.fold_in(key, 6), axis_at), (shards_of,), jnp.float32, low / len(split), largest / len(split))
        level = level * jnp.repeat(jnp.exp(heights), extent[axis_at] // shards_of).reshape((-1,) + (1,) * (len(extent) - 1 - axis_at))
    return level


def normal_values(own_key, extent, scale, reach, shards=(), held_as=jnp.bfloat16):
    drawn = jax.random.normal(own_key, extent, jnp.float32) * scale
    if len(shards) > 0:
        drawn = block_levels(own_key, extent, shards, -0.22, 0.18) * drawn
    return jnp.clip(drawn, min=-reach, max=reach).astype(held_as)


def setup_inputs(seed: int = 0) -> dict:
    splits = jax.random.split(jax.random.key(seed), 6)
    queries = draw_queries(jax.random.fold_in(splits[5], 71), 0)
    keys = draw_keys(jax.random.fold_in(splits[5], 71), 0)
    values = draw_values(jax.random.fold_in(splits[5], 71), 0)
    grad_out = normal_values(splits[3], (SEQS, SEQ_LEN, D), 0.5, 3.0, ((0, 4), (1, 32)))
    w_out = normal_values(splits[4], (D, D), D ** -0.5, 0.1875)
    return {"queries": queries, "keys": keys, "values": values, "grad_out": grad_out, "w_out": w_out}


LOG_TWO = math.log(2.0)

def pooled(rows):
    shape = rows.shape
    pairs = rows.astype(jnp.float32).reshape(shape[:-2] + (shape[-2] // 2, 2, shape[-1]))
    return ((pairs[..., 0, :] + pairs[..., 1, :]) * 0.5).astype(jnp.bfloat16)

def sibling(blocks):
    count = blocks.shape[0]
    return jnp.flip(blocks.reshape((count // 2, 2) + blocks.shape[1:]), axis=1).reshape(blocks.shape)

def grouped(per_token, groups):
    return jnp.transpose(per_token.reshape(groups, -1, per_token.shape[-1]), (0, 2, 1))

def ungrouped(blocks):
    return jnp.transpose(blocks, (0, 2, 1)).reshape(-1, blocks.shape[1])

def widened(narrow):
    return lax.optimization_barrier(narrow).astype(jnp.float32)

def level_blocks(level, query_rows, key_rows, value_rows):
    if level == 0:
        shape = (query_rows.shape[0] // (2 * BLOCK), 2 * BLOCK, HEADS, HEAD_DIM)
        return (query_rows.reshape(shape), key_rows.reshape(shape), value_rows.reshape(shape))
    shape = (query_rows.shape[0] // BLOCK, BLOCK, HEADS, HEAD_DIM)
    return (query_rows.reshape(shape), sibling(key_rows.reshape(shape)), sibling(value_rows.reshape(shape)))

def level_scores(level, query_blocks, key_blocks):
    scale = 1.0 / math.sqrt(HEAD_DIM)
    scores = jnp.einsum('gqhd,gkhd->ghqk', query_blocks.astype(jnp.float32), key_blocks.astype(jnp.float32))
    return jnp.repeat(scores * scale + level * LOG_TWO, 2 ** level, axis=2)

def one_sequence(query_tok, key_tok, value_tok, grad_tok, w_out):
    scale = 1.0 / math.sqrt(HEAD_DIM)
    pyramid = [(query_tok, key_tok, value_tok)]
    for level in range(1, LEVELS):
        previous = pyramid[-1]
        pyramid.append((pooled(previous[0]), pooled(previous[1]), pooled(previous[2])))
    top = None
    for level in range(LEVELS):
        query_blocks, key_blocks, value_blocks = level_blocks(level, *pyramid[level])
        row_top = ungrouped(lax.optimization_barrier(jnp.max(level_scores(level, query_blocks, key_blocks), axis=3)))
        top = row_top if top is None else jnp.maximum(top, row_top)
    numer = jnp.zeros((SEQ_LEN, HEADS, HEAD_DIM), jnp.float32)
    denom = jnp.zeros((SEQ_LEN, HEADS), jnp.float32)
    for level in range(LEVELS):
        query_blocks, key_blocks, value_blocks = level_blocks(level, *pyramid[level])
        scores = level_scores(level, query_blocks, key_blocks)
        groups = scores.shape[0]
        expo = jnp.exp(scores - grouped(top, groups)[..., None])
        term = jnp.einsum('ghrk,gkhd->grhd', widened(expo.astype(jnp.bfloat16)), value_blocks.astype(jnp.float32))
        numer = numer + term.reshape(SEQ_LEN, HEADS, HEAD_DIM)
        denom = denom + ungrouped(lax.optimization_barrier(jnp.sum(expo, axis=3)))
    attended = (numer / denom[:, :, None]).reshape(SEQ_LEN, D).astype(jnp.bfloat16)
    mixed = jnp.dot(attended, w_out, preferred_element_type=jnp.float32).astype(jnp.bfloat16)
    grad_att = jnp.dot(grad_tok, w_out.T, preferred_element_type=jnp.float32).astype(jnp.bfloat16)
    weight_term = jnp.dot(attended.T, grad_tok, preferred_element_type=jnp.float32)
    delta = lax.optimization_barrier(jnp.sum(grad_att.astype(jnp.float32).reshape(SEQ_LEN, HEADS, HEAD_DIM) * attended.astype(jnp.float32).reshape(SEQ_LEN, HEADS, HEAD_DIM), axis=2))
    query_grads = [jnp.zeros((SEQ_LEN // 2 ** level, D), jnp.float32) for level in range(LEVELS)]
    key_grads = [jnp.zeros((SEQ_LEN // 2 ** level, D), jnp.float32) for level in range(LEVELS)]
    value_grads = [jnp.zeros((SEQ_LEN // 2 ** level, D), jnp.float32) for level in range(LEVELS)]
    for level in range(LEVELS):
        query_blocks, key_blocks, value_blocks = level_blocks(level, *pyramid[level])
        scores = level_scores(level, query_blocks, key_blocks)
        groups = scores.shape[0]
        prob = jnp.exp(scores - grouped(top, groups)[..., None]) / grouped(denom, groups)[..., None]
        grad_rows = grad_att.reshape(groups, -1, HEADS, HEAD_DIM).astype(jnp.float32)
        value_grad = jnp.einsum('ghrk,grhd->gkhd', widened(prob.astype(jnp.bfloat16)), grad_rows)
        prob_grad = jnp.einsum('grhd,gkhd->ghrk', grad_rows, value_blocks.astype(jnp.float32))
        score_grad = prob * (prob_grad - grouped(delta, groups)[..., None])
        summed = score_grad.reshape(groups, HEADS, -1, 2 ** level, score_grad.shape[3]).sum(axis=3)
        summed = widened(summed.astype(jnp.bfloat16))
        query_grad = jnp.einsum('ghqk,gkhd->gqhd', summed, key_blocks.astype(jnp.float32)) * scale
        key_grad = jnp.einsum('ghqk,gqhd->gkhd', summed, query_blocks.astype(jnp.float32)) * scale
        if level > 0:
            key_grad = sibling(key_grad)
            value_grad = sibling(value_grad)
        query_grads[level] = query_grads[level] + query_grad.reshape(-1, D)
        key_grads[level] = key_grads[level] + key_grad.reshape(-1, D)
        value_grads[level] = value_grads[level] + value_grad.reshape(-1, D)
    for level in range(LEVELS - 1, 0, -1):
        query_grads[level - 1] = query_grads[level - 1] + 0.5 * jnp.repeat(query_grads[level], 2, axis=0)
        key_grads[level - 1] = key_grads[level - 1] + 0.5 * jnp.repeat(key_grads[level], 2, axis=0)
        value_grads[level - 1] = value_grads[level - 1] + 0.5 * jnp.repeat(value_grads[level], 2, axis=0)
    return (mixed, query_grads[0].astype(jnp.bfloat16), key_grads[0].astype(jnp.bfloat16), value_grads[0].astype(jnp.bfloat16), weight_term)

def reference(queries, keys, values, grad_out, w_out):
    results = []
    for sequence in range(SEQS):
        results.append(one_sequence(queries[sequence], keys[sequence], values[sequence], grad_out[sequence], w_out))
    mixed = jnp.stack([item[0] for item in results])
    grad_queries = jnp.stack([item[1] for item in results])
    grad_keys = jnp.stack([item[2] for item in results])
    grad_values = jnp.stack([item[3] for item in results])
    weight_total = results[0][4]
    for item in results[1:]:
        weight_total = weight_total + item[4]
    grad_w_out = weight_total * (1.0 / math.sqrt(SEQS * SEQ_LEN))
    return (mixed, grad_queries, grad_keys, grad_values, grad_w_out)
```

```python
import math

import jax
import jax.numpy as jnp
from jax import lax
from jax.experimental import pallas as pl
from jax.experimental.pallas import tpu as pltpu
from jax.sharding import PartitionSpec as P

HEADS = 8
HD = 128
TOK = 256
D = 1024
ROWS = {1: 128, 2: 64, 3: 32, 4: 16, 5: 8}
SCALE = 1.0 / math.sqrt(HD)
LOG_TWO = math.log(2.0)
F32 = jnp.float32
BF16 = jnp.bfloat16
MESH = pl.DeviceIdType.MESH
CORE, X1, X3, Z1, Z3 = 1, 2, 6, 8, 24


def dot(a, b, ca=1, cb=0):
    return lax.dot_general(a, b, (((ca,), (cb,)), ((), ())), preferred_element_type=F32)


def twice(x):
    return jnp.concatenate([x, x], axis=0)


def fold(x):
    n = x.shape[0] // 2
    return x[:n] + x[n:]


def wide(x, lanes=HD):
    return jnp.broadcast_to(x, (x.shape[0], lanes))


SCRATCH = {
    "raw": ((4, TOK, D), BF16),
    "w": ((D, D), BF16),
    "perm": ((TOK, TOK), BF16),
    "back": ((TOK, TOK), BF16),
    "tok": ((4, TOK, D), BF16),
    "ga": ((TOK, D), BF16),
    "att": ((TOK, D), BF16),
    "own1": ((2, 128, D), BF16),
    "own2": ((2, 64, D), BF16),
    "own3": ((2, 32, D), BF16),
    "own4": ((2, 16, D), BF16),
    "own5": ((16, D), BF16),
    "q1": ((128, D), BF16),
    "q2": ((64, D), BF16),
    "q3": ((32, D), BF16),
    "q4": ((16, D), BF16),
    "q5": ((8, D), BF16),
    "sib1": ((2, 128, D), BF16),
    "sib2": ((2, 128, D), BF16),
    "sib3": ((2, 128, D), BF16),
    "sib4": ((2, 128, D), BF16),
    "land5": ((16, 16, D), BF16),
    "sib5": ((2, 128, D), BF16),
    "e0": ((HEADS, TOK, TOK), BF16),
    "n0": ((HEADS, TOK, HD), F32),
    "m0": ((HEADS, TOK, HD), F32),
    "d0": ((HEADS, TOK, HD), F32),
    "gam": ((HEADS, TOK, HD), F32),
    "del": ((HEADS, TOK, HD), F32),
    "kv0": ((2, TOK, D), F32),
    "fin": ((2, TOK, D), BF16),
    "dq": ((TOK, D), BF16),
    "out": ((4, TOK, D), BF16),
    "gown": ((D, 512), F32),
    "g0s": ((D, 512), BF16),
    "g0r": ((D, 512), BF16),
    "ga1s": ((4, 256, 256), BF16),
    "ga1r": ((3, 256, 256), BF16),
    "ga2s": ((4, 64, 256), BF16),
    "ga2r": ((3, 64, 256), BF16),
    "ga2f": ((4, 64, 256), F32),
    "gb1s": ((4, 4, 64, 256), BF16),
    "gb1r": ((3, 4, 64, 256), BF16),
    "gb2s": ((4, 64, 256), BF16),
    "gb2r": ((3, 64, 256), BF16),
    "gb2f": ((4, 64, 256), F32),
    "gc1s": ((4, 16, 512), BF16),
    "gc1r": ((3, 16, 512), BF16),
    "gc1f": ((4, 16, 512), F32),
    "gds": ((2, 8, 512), F32),
    "gdr": ((8, 512), F32),
    "gout": ((8, D), F32),
}
for _l, _n in ROWS.items():
    SCRATCH["e%d" % _l] = ((HEADS, _n, HD), F32)
    SCRATCH["n%d" % _l] = ((HEADS, _n, HD), F32)
    SCRATCH["m%d" % _l] = ((HEADS, _n, HD), F32)
    SCRATCH["d%d" % _l] = ((HEADS, _n, HD), F32)
    SCRATCH["g%d" % _l] = ((HEADS, _n, HD), F32)
    SCRATCH["t%d" % _l] = ((HEADS, _n, HD), F32)
    SCRATCH["dq%d" % _l] = ((_n, D), F32)
BACK = {
    1: ((CORE, 128),),
    2: ((CORE, 64), (X1, 64)),
    3: ((CORE, 64), (X1, 32), (X3, 32)),
    4: ((CORE, 64), (X3, 32), (X1, 16), (Z1, 16)),
    5: ((CORE, 64), (X3, 32), (X1, 16), (Z1, 8), (Z3, 8)),
}
for _l, _rounds in BACK.items():
    for _i, (_p, _n) in enumerate(_rounds):
        _shape = (_n // 8, 16, D) if _l == 5 else (2, _n, D)
        SCRATCH["bs%d_%d" % (_l, _i)] = (_shape, BF16)
        SCRATCH["br%d_%d" % (_l, _i)] = (_shape, BF16)
    if _l > 1:
        SCRATCH["acc%d" % _l] = ((8, 16, D) if _l == 5 else (2, 64, D), F32)
NAMES = list(SCRATCH)
COPIES = 80


def kernel(q_in, k_in, v_in, g_in, w_in, mixed_o, gq_o, gk_o, gv_o, gw_o, *scratch):
    s = dict(zip(NAMES, scratch[: len(NAMES)]))
    ssem, rsem, lsem = scratch[len(NAMES) :]
    dp = lax.axis_index("dp")
    me = lax.axis_index("seq")
    core = me % 2
    x_at = (me // 2) % 4
    z_at = me // 8

    def flipped(bits):
        out = me
        for bit in range(5):
            if bits >> bit & 1:
                out = out + (1 - 2 * ((me // 2**bit) % 2)) * 2**bit
        return out

    def flip2(at, k):
        out = at
        for bit in range(2):
            if k >> bit & 1:
                out = out + (1 - 2 * ((at // 2**bit) % 2)) * 2**bit
        return out

    peers = [(dp, flipped(b)) for b in (1, 2, 4, 6, 8, 16, 24)]
    peers += [(flip2(dp, k), me) for k in (1, 2, 3)]
    barrier = pltpu.get_barrier_semaphore()
    for peer in peers:
        pl.semaphore_signal(barrier, inc=1, device_id=peer, device_id_type=MESH)

    loads = []
    for i, src in enumerate((k_in, v_in, q_in, g_in)):
        loads.append(pltpu.make_async_copy(src, s["raw"].at[i], lsem.at[i]))
    loads.append(pltpu.make_async_copy(w_in, s["w"], lsem.at[4]))
    for load in loads:
        load.start()

    sent = []
    counter = [0]
    by_name = {}

    def send(name, src, dst, device):
        i = counter[0]
        counter[0] += 1
        copy = pltpu.make_async_remote_copy(
            src_ref=src,
            dst_ref=dst,
            send_sem=ssem.at[i],
            recv_sem=rsem.at[i],
            device_id=device,
            device_id_type=MESH,
        )
        copy.start()
        sent.append(copy)
        by_name[name] = copy

    def got(name):
        by_name[name].wait_recv()

    def to(bits):
        return (dp, flipped(bits))

    def source(p):
        r = p // 8
        rev = (r % 2) * 16 + (r // 2 % 2) * 8 + (r // 4 % 2) * 4 + (r // 8 % 2) * 2 + r // 16
        return (p % 8) * 32 + rev

    rows = lax.broadcasted_iota(jnp.int32, (TOK, TOK), 0)
    cols = lax.broadcasted_iota(jnp.int32, (TOK, TOK), 1)
    s["perm"][...] = (cols == source(rows)).astype(F32).astype(BF16)
    s["back"][...] = (rows == source(cols)).astype(F32).astype(BF16)

    def loop(n, f):
        def step(i, carry):
            f(i)
            return carry

        lax.fori_loop(0, n, step, 0)

    def at(i, width=HD):
        return pl.ds(pl.multiple_of(i * width, width), width)

    def reorder(i):
        def chunk(c):
            s["tok"][i, :, at(c, 256)] = dot(s["perm"][...], s["raw"][i, :, at(c, 256)]).astype(BF16)

        loop(4, chunk)

    def halves(x):
        return (fold(x.astype(F32)) * 0.5).astype(BF16)

    loads[0].wait()
    reorder(0)
    loads[1].wait()
    reorder(1)

    def pyramid(c):
        fives = []
        for i in range(2):
            x = s["tok"][i, :, at(c, 256)]
            for level in range(1, 5):
                x = halves(x)
                s["own%d" % level][i, :, at(c, 256)] = x
            fives.append(fold(x.astype(F32)) * 0.5)
        s["own5"][:, at(c, 256)] = jnp.concatenate(fives, axis=0).astype(BF16)

    loop(4, pyramid)
    pl.semaphore_wait(barrier, len(peers))
    send("f5z3", s["own5"], s["land5"].at[0], to(Z3))
    send("f4z1", s["own4"], s["sib4"].at[:, pl.ds(0, 16)], to(Z1))
    send("f3x3", s["own3"], s["sib3"].at[:, pl.ds(0, 32)], to(X3))
    send("f2x1", s["own2"], s["sib2"].at[:, pl.ds(0, 64)], to(X1))
    send("f1", s["own1"], s["sib1"], to(CORE))

    def relay(name, was, level, n, bits):
        got(was)
        if level == 5:
            g = n // 8
            send(name, s["land5"].at[pl.ds(0, g)], s["land5"].at[pl.ds(g, g)], to(bits))
        else:
            ref = s["sib%d" % level]
            send(name, ref.at[:, pl.ds(0, n)], ref.at[:, pl.ds(n, n)], to(bits))

    loads[2].wait()
    reorder(2)

    def q_pyramid(c):
        x = s["tok"][2, :, at(c, 256)]
        for level in range(1, 6):
            y = fold(x.astype(F32)) * 0.5
            x = y.astype(BF16)
            s["q%d" % level][:, at(c, 256)] = x

    loop(4, q_pyramid)
    loads[3].wait()
    reorder(3)
    relay("f5z1", "f5z3", 5, 8, Z1)
    relay("f4x1", "f4z1", 4, 16, X1)
    relay("f3x1", "f3x3", 3, 32, X1)
    loads[4].wait()

    def grad_att(c):
        s["ga"][:, at(c, 256)] = dot(s["tok"][3], s["w"][at(c, 256), :], 1, 1).astype(BF16)

    loop(4, grad_att)
    relay("f5x1", "f5z1", 5, 16, X1)
    relay("f2c", "f2x1", 2, 64, CORE)
    relay("f4x3", "f4x1", 4, 32, X3)

    def zero_forward(h):
        sc = dot(s["tok"][2, :, at(h)], s["tok"][0, :, at(h)], 1, 1) * SCALE
        m = jnp.max(sc, axis=1, keepdims=True)
        e = jnp.exp(sc - m)
        s["d0"][h] = wide(jnp.sum(e, axis=1, keepdims=True))
        s["m0"][h] = wide(m)
        eb = e.astype(BF16)
        s["e0"][h] = eb
        s["n0"][h] = dot(eb, s["tok"][1, :, at(h)])

    loop(4, zero_forward)
    relay("f3c", "f3x1", 3, 64, CORE)
    relay("f5x3", "f5x1", 5, 32, X3)
    loop(4, lambda h: zero_forward(h + 4))
    relay("f4c", "f4x3", 4, 64, CORE)

    def coarse_forward(level):
        def head(h):
            sc = dot(s["q%d" % level][:, at(h)], s["sib%d" % level][0, :, at(h)], 1, 1)
            sc = sc * SCALE + level * LOG_TWO
            m = jnp.max(sc, axis=1, keepdims=True)
            e = jnp.exp(sc - m)
            s["d%d" % level][h] = wide(jnp.sum(e, axis=1, keepdims=True))
            s["m%d" % level][h] = wide(m)
            s["e%d" % level][h] = e
            s["n%d" % level][h] = dot(e.astype(BF16), s["sib%d" % level][1, :, at(h)])

        loop(HEADS, head)

    got("f1")
    coarse_forward(1)
    relay("f5c", "f5x3", 5, 64, CORE)
    got("f2c")
    coarse_forward(2)
    got("f3c")
    coarse_forward(3)
    got("f4c")
    coarse_forward(4)
    got("f5c")

    def unpack5(h):
        x = s["land5"][:, :, at(h)].astype(F32)
        s["sib5"][0, :, at(h)] = x[:, :8].reshape(128, HD).astype(BF16)
        s["sib5"][1, :, at(h)] = x[:, 8:].reshape(128, HD).astype(BF16)

    loop(HEADS, unpack5)
    coarse_forward(5)

    def merge(h):
        c, num, den = s["m5"][h], s["n5"][h], s["d5"][h]
        a, b = {}, {}
        for level in (4, 3, 2, 1):
            m = s["m%d" % level][h]
            spread = twice(c)
            c = jnp.maximum(m, spread)
            a[level] = jnp.exp(m - c)
            b[level] = jnp.exp(spread - c)
            num = s["n%d" % level][h] * a[level] + twice(num) * b[level]
            den = s["d%d" % level][h] * a[level] + twice(den) * b[level]
        m = s["m0"][h]
        spread = twice(c)
        c = jnp.maximum(m, spread)
        a0 = jnp.exp(m - c)
        b0 = jnp.exp(spread - c)
        num = s["n0"][h] * a0 + twice(num) * b0
        den = s["d0"][h] * a0 + twice(den) * b0
        inv = 1.0 / den
        att = (num * inv).astype(BF16)
        s["att"][:, at(h)] = att
        ga = s["ga"][:, at(h)].astype(F32)
        delta = wide(jnp.sum(ga * att.astype(F32), axis=1, keepdims=True))
        s["gam"][h] = a0 * inv
        s["del"][h] = delta
        weight = b0 * inv
        grad = fold(weight * ga)
        diff = fold(weight * delta)
        for level in range(1, 6):
            if level < 5:
                s["g%d" % level][h] = grad * a[level]
                s["t%d" % level][h] = diff * a[level]
                grad = fold(grad * b[level])
                diff = fold(diff * b[level])
            else:
                s["g5"][h] = grad
                s["t5"][h] = diff

    loop(HEADS, merge)

    other = 1 - core

    def weight_other(h):
        cols = pl.ds(pl.multiple_of(other * 512, 512), 512)
        s["g0s"][at(h), :] = dot(s["att"][:, at(h)], s["tok"][3, :, cols], 0, 0).astype(BF16)

    loop(HEADS, weight_other)
    send("g0", s["g0s"], s["g0r"], to(CORE))

    def coarse_backward(level):
        def head(h):
            key, value = s["sib%d" % level][0, :, at(h)], s["sib%d" % level][1, :, at(h)]
            grad = s["g%d" % level][h].astype(BF16)
            e = s["e%d" % level][h]
            ds = e * (dot(grad, value, 1, 1) - s["t%d" % level][h])
            ds = ds.astype(BF16)
            s["dq%d" % level][:, at(h)] = dot(ds, key) * SCALE
            dk = dot(ds, s["q%d" % level][:, at(h)], 0, 0) * SCALE
            dv = dot(e.astype(BF16), grad, 0, 0)
            if level == 1:
                s["bs1_0"][0, :, at(h)] = dk.astype(BF16)
                s["bs1_0"][1, :, at(h)] = dv.astype(BF16)
            elif level < 5:
                for i, x in enumerate((dk, dv)):
                    s["acc%d" % level][i, :, at(h)] = x[:64]
                    s["bs%d_0" % level][i, :, at(h)] = x[64:].astype(BF16)
            else:
                pair = jnp.concatenate([dk.reshape(16, 8, HD), dv.reshape(16, 8, HD)], axis=1)
                s["acc5"][:, :, at(h)] = pair[:8]
                s["bs5_0"][:, :, at(h)] = pair[8:].astype(BF16)

        loop(HEADS, head)
        send("b%d_0" % level, s["bs%d_0" % level], s["br%d_0" % level], to(CORE))

    def back_step(level, i):
        got("b%d_%d" % (level, i - 1))
        rounds = BACK[level]
        bits, n = rounds[i]
        held = rounds[i - 1][1]
        acc, came, out = (s[x % level] for x in ("acc%d", "br%%d_%d" % (i - 1), "bs%%d_%d" % i))

        def chunk(c):
            if level == 5:
                total = acc[: held // 8, :, at(c, 256)] + came[:, :, at(c, 256)].astype(F32)
                keep = (held - n) // 8
                out[:, :, at(c, 256)] = total[keep:].astype(BF16)
                if keep:
                    acc[:keep, :, at(c, 256)] = total[:keep]
            else:
                keep = held - n
                for j in range(2):
                    total = acc[j, :held, at(c, 256)] + came[j, :, at(c, 256)].astype(F32)
                    out[j, :, at(c, 256)] = total[keep:].astype(BF16)
                    if keep:
                        acc[j, :keep, at(c, 256)] = total[:keep]

        loop(4, chunk)
        send("b%d_%d" % (level, i), out, s["br%d_%d" % (level, i)], to(bits))

    coarse_backward(2)

    def weight_own(h):
        cols = pl.ds(pl.multiple_of(core * 512, 512), 512)
        s["gown"][at(h), :] = dot(s["att"][:, at(h)], s["tok"][3, :, cols], 0, 0)

    loop(HEADS, weight_own)
    back_step(2, 1)
    got("g0")

    def weight_sum(j):
        x = s["gown"][at(j, 64), :] + s["g0r"][at(j, 64), :].astype(F32)
        s["gown"][at(j, 64), :] = x
        s["ga1s"][j // 4, pl.ds(pl.multiple_of((j % 4) * 64, 64), 64), :] = x[:, :256].astype(BF16)
        s["gb1s"][j // 4, j % 4] = x[:, 256:].astype(BF16)

    loop(16, weight_sum)
    y_dev = [(flip2(dp, k), me) for k in (1, 2, 3)]
    z_dev = [(dp, flipped(8 * k)) for k in (1, 2, 3)]
    x_dev = [(dp, flipped(2 * k)) for k in (1, 2, 3)]
    for k in (1, 2, 3):
        send("ga1_%d" % k, s["ga1s"].at[flip2(dp, k)], s["ga1r"].at[k - 1], y_dev[k - 1])
        send("gb1_%d" % k, s["gb1s"].at[:, flip2(z_at, k)], s["gb1r"].at[k - 1], z_dev[k - 1])

    coarse_backward(5)
    coarse_backward(4)
    back_step(5, 1)
    coarse_backward(3)
    back_step(4, 1)
    back_step(3, 1)
    coarse_backward(1)
    back_step(5, 2)
    back_step(4, 2)

    def zero_backward(h):
        e = s["e0"][h]
        q, ga = s["tok"][2, :, at(h)], s["ga"][:, at(h)]
        k, v = s["tok"][0, :, at(h)], s["tok"][1, :, at(h)]
        gam, delta = s["gam"][h], s["del"][h]
        both = jnp.concatenate([delta, delta], axis=1)
        ds = (e.astype(F32) * (dot(ga, v, 1, 1) - both)).astype(BF16)
        gq = (q.astype(F32) * gam).astype(BF16)
        gg = (ga.astype(F32) * gam).astype(BF16)
        s["kv0"][0, :, at(h)] = dot(ds, gq, 0, 0) * SCALE
        s["kv0"][1, :, at(h)] = dot(e, gg, 0, 0)
        up = s["dq5"][:, at(h)]
        for level in (4, 3, 2, 1):
            up = s["dq%d" % level][:, at(h)] + 0.5 * twice(up)
        dq = dot(ds, k) * gam * SCALE + 0.5 * twice(up)
        s["dq"][:, at(h)] = dq.astype(BF16)

    loop(4, zero_backward)
    back_step(3, 2)
    back_step(4, 3)
    back_step(5, 3)

    def weight_first():
        for k in (1, 2, 3):
            got("ga1_%d" % k)
            got("gb1_%d" % k)

        def chunk(j):
            r = pl.ds(pl.multiple_of(dp * 256 + j * 64, 64), 64)
            x = s["gown"][r, :256]
            for k in range(3):
                x = x + s["ga1r"][k, at(j, 64), :].astype(F32)
            s["ga2f"][j] = x
            s["ga2s"][j] = x.astype(BF16)
            r = pl.ds(pl.multiple_of(j * 256 + z_at * 64, 64), 64)
            x = s["gown"][r, 256:]
            for k in range(3):
                x = x + s["gb1r"][k, j].astype(F32)
            s["gb2f"][j] = x
            s["gb2s"][j] = x.astype(BF16)

        loop(4, chunk)
        for k in (1, 2, 3):
            send("ga2_%d" % k, s["ga2s"].at[flip2(z_at, k)], s["ga2r"].at[k - 1], z_dev[k - 1])
            send("gb2_%d" % k, s["gb2s"].at[flip2(dp, k)], s["gb2r"].at[k - 1], y_dev[k - 1])

    loop(2, lambda h: zero_backward(h + 4))
    weight_first()
    loop(2, lambda h: zero_backward(h + 6))
    back_step(5, 4)

    stores = []

    def store(i, out):
        copy = pltpu.make_async_copy(s["out"].at[i], out, lsem.at[5 + i])
        copy.start()
        stores.append(copy)

    def ordered(i, src):
        def chunk(c):
            s["out"][i, :, at(c, 256)] = dot(s["back"][...], src(c)).astype(BF16)

        loop(4, chunk)

    ordered(1, lambda c: s["dq"][:, at(c, 256)])
    store(1, gq_o)

    def weight_second():
        for k in (1, 2, 3):
            got("ga2_%d" % k)
            got("gb2_%d" % k)
        a = s["ga2f"][z_at]
        b = s["gb2f"][dp]
        for k in range(3):
            a = a + s["ga2r"][k].astype(F32)
            b = b + s["gb2r"][k].astype(F32)
        x = jnp.concatenate([a, b], axis=1).reshape(4, 16, 512)
        s["gc1f"][...] = x
        s["gc1s"][...] = x.astype(BF16)
        for k in (1, 2, 3):
            send("gc1_%d" % k, s["gc1s"].at[flip2(x_at, k)], s["gc1r"].at[k - 1], x_dev[k - 1])

    weight_second()
    ordered(0, lambda c: dot(s["att"][...], s["w"][:, at(c, 256)]).astype(BF16))
    store(0, mixed_o)

    for k in (1, 2, 3):
        got("gc1_%d" % k)
    x = s["gc1f"][x_at]
    for k in range(3):
        x = x + s["gc1r"][k].astype(F32)
    s["gds"][0] = x[:8]
    s["gds"][1] = x[8:]
    send("gd", s["gds"].at[other], s["gdr"], to(CORE))

    for level in range(1, 6):
        got("b%d_%d" % (level, len(BACK[level]) - 1))

    def finish(h):
        for i in range(2):
            up = s["br5_4"][0, :, at(h)].astype(F32)[8 * i : 8 * i + 8]
            for level in (4, 3, 2, 1):
                own = s["br%d_%d" % (level, len(BACK[level]) - 1)][i, :, at(h)]
                up = own.astype(F32) + 0.5 * twice(up)
            up = s["kv0"][i, :, at(h)] + 0.5 * twice(up)
            s["fin"][i, :, at(h)] = up.astype(BF16)

    loop(HEADS, finish)
    ordered(2, lambda c: s["fin"][0, :, at(c, 256)])
    store(2, gk_o)
    ordered(3, lambda c: s["fin"][1, :, at(c, 256)])
    store(3, gv_o)

    factor = 1.0 / math.sqrt(4 * 8192)
    got("gd")
    mine = s["gds"][core]
    s["gout"][:, pl.ds(pl.multiple_of(core * 512, 512), 512)] = mine * factor
    s["gout"][:, pl.ds(pl.multiple_of(other * 512, 512), 512)] = s["gdr"][...] * factor
    last = pltpu.make_async_copy(s["gout"], gw_o, lsem.at[9])
    last.start()
    for copy in sent:
        copy.wait_send()
    for copy in stores:
        copy.wait()
    last.wait()


def body(queries, keys, values, grad_out, w_out):
    shape = jax.ShapeDtypeStruct((TOK, D), BF16)
    outs = pl.pallas_call(
        kernel,
        out_shape=(shape, shape, shape, shape, jax.ShapeDtypeStruct((8, D), F32)),
        in_specs=[pl.BlockSpec(memory_space=pl.ANY)] * 5,
        out_specs=[pl.BlockSpec(memory_space=pl.ANY)] * 5,
        scratch_shapes=[pltpu.VMEM(*SCRATCH[name]) for name in NAMES]
        + [
            pltpu.SemaphoreType.DMA((COPIES,)),
            pltpu.SemaphoreType.DMA((COPIES,)),
            pltpu.SemaphoreType.DMA((10,)),
        ],
        compiler_params=pltpu.CompilerParams(
            collective_id=0, has_side_effects=True, vmem_limit_bytes=60 * 1024 * 1024
        ),
    )(queries[0], keys[0], values[0], grad_out[0], w_out)
    return tuple(out[None] for out in outs[:4]) + (outs[4],)


def solution(mesh):
    tokens = P("dp", "seq", None)
    return jax.shard_map(
        body,
        mesh=mesh,
        in_specs=(tokens, tokens, tokens, tokens, P()),
        out_specs=(tokens, tokens, tokens, tokens, P(("dp", "seq"), None)),
        check_vma=False,
    )
```

```python
import math

import jax
import jax.numpy as jnp
from jax import lax
from jax.experimental import pallas as pl
from jax.experimental.pallas import tpu as pltpu
from jax.sharding import PartitionSpec as P

HEADS = 8
HD = 128
TOK = 256
D = 1024
ROWS = {1: 128, 2: 64, 3: 32, 4: 16, 5: 8}
SCALE = 1.0 / math.sqrt(HD)
LOG_TWO = math.log(2.0)
F32 = jnp.float32
BF16 = jnp.bfloat16
MESH = pl.DeviceIdType.MESH
CORE, X1, X3, Z1, Z2, Z3 = 1, 2, 6, 8, 16, 24


def dot(a, b, ca=1, cb=0):
    return lax.dot_general(a, b, (((ca,), (cb,)), ((), ())), preferred_element_type=F32)


def twice(x):
    return jnp.concatenate([x, x], axis=0)


def fold(x):
    n = x.shape[0] // 2
    return x[:n] + x[n:]


def wide(x, lanes=HD):
    return jnp.broadcast_to(x, (x.shape[0], lanes))


SCRATCH = {
    "raw": ((4, TOK, D), BF16),
    "w": ((D, D), BF16),
    "perm": ((TOK, TOK), BF16),
    "tok": ((4, TOK, D), BF16),
    "ga": ((TOK, D), BF16),
    "att": ((TOK, D), BF16),
    "own1": ((2, 128, D), BF16),
    "own2": ((2, 64, D), BF16),
    "own3": ((2, 32, D), BF16),
    "own4": ((2, 16, D), BF16),
    "own5": ((16, D), BF16),
    "q1": ((128, D), BF16),
    "q2": ((64, D), BF16),
    "q3": ((32, D), BF16),
    "q4": ((16, D), BF16),
    "q5": ((8, D), BF16),
    "sib1": ((2, 128, D), BF16),
    "sib2": ((2, 128, D), BF16),
    "sib3": ((2, 128, D), BF16),
    "sib4": ((2, 128, D), BF16),
    "land5": ((16, 16, D), BF16),
    "sib5": ((2, 128, D), BF16),
    "e0": ((HEADS, TOK, TOK), BF16),
    "n0": ((HEADS, TOK, HD), F32),
    "m0": ((HEADS, TOK, HD), F32),
    "d0": ((HEADS, TOK, HD), F32),
    "gam": ((HEADS, TOK, HD), F32),
    "del": ((HEADS, TOK, HD), F32),
    "kv0": ((2, TOK, D), F32),
    "fin": ((2, TOK, D), BF16),
    "dq": ((TOK, D), BF16),
    "mixed": ((TOK, D), BF16),
    "gown": ((D, 512), F32),
    "g0s": ((D, 512), BF16),
    "g0r": ((D, 512), BF16),
    "ga1s": ((4, 256, 256), BF16),
    "ga1r": ((3, 256, 256), BF16),
    "ga2s": ((4, 64, 256), BF16),
    "ga2r": ((3, 64, 256), BF16),
    "ga2f": ((4, 64, 256), F32),
    "gb1s": ((4, 4, 64, 256), BF16),
    "gb1r": ((3, 4, 64, 256), BF16),
    "gb2s": ((4, 64, 256), BF16),
    "gb2r": ((3, 64, 256), BF16),
    "gb2f": ((4, 64, 256), F32),
    "gc1s": ((4, 16, 512), BF16),
    "gc1r": ((3, 16, 512), BF16),
    "gc1f": ((4, 16, 512), F32),
    "gds": ((2, 8, 512), F32),
    "gdr": ((8, 512), F32),
    "gout": ((8, D), F32),
}
for _l, _n in ROWS.items():
    for _c in "enmdgt":
        SCRATCH["%s%d" % (_c, _l)] = ((HEADS * _n, HD), F32)
    SCRATCH["dq%d" % _l] = ((_n, D), F32)
BACK = {
    1: ((CORE, 128),),
    2: ((CORE, 64), (X1, 64)),
    3: ((CORE, 64), (X1, 32), (X3, 32)),
    4: ((CORE, 64), (X3, 32), (X1, 16), (Z1, 16)),
    5: ((CORE, 64), (X3, 32), (X1, 16), (Z3, 8), (Z2, 8)),
}
for _l, _rounds in BACK.items():
    for _i, (_p, _n) in enumerate(_rounds):
        _shape = (_n // 8, 16, D) if _l == 5 else (2, _n, D)
        SCRATCH["bs%d_%d" % (_l, _i)] = (_shape, BF16)
        SCRATCH["br%d_%d" % (_l, _i)] = (_shape, BF16)
    if _l > 1:
        SCRATCH["acc%d" % _l] = ((8, 16, D) if _l == 5 else (2, 64, D), F32)
NAMES = list(SCRATCH)
COPIES = 80


def source(p):
    r = p // 8
    rev = (r % 2) * 16 + (r // 2 % 2) * 8 + (r // 4 % 2) * 4 + (r // 8 % 2) * 2 + r // 16
    return (p % 8) * 32 + rev


def reordering(axis):
    at = lax.broadcasted_iota(jnp.int32, (TOK, TOK), axis)
    token = lax.broadcasted_iota(jnp.int32, (TOK, TOK), 1 - axis)
    return (token == source(at)).astype(F32).astype(BF16)


def restore(rows_in, gw_in, mixed_o, gq_o, gk_o, gv_o, gw_o, held, out, gw, sem):
    loads = [pltpu.make_async_copy(rows_in.at[i], held.at[i], sem.at[i]) for i in range(4)]
    loads.append(pltpu.make_async_copy(gw_in, gw, sem.at[4]))
    for load in loads:
        load.start()
    back = reordering(1)
    stores = []
    for i, target in enumerate((mixed_o, gq_o, gk_o, gv_o)):
        loads[i].wait()
        for c in range(4):
            cols = pl.ds(c * 256, 256)
            out[i, :, cols] = dot(back, held[i, :, cols]).astype(BF16)
        stores.append(pltpu.make_async_copy(out.at[i], target, sem.at[5 + i]))
        stores[-1].start()
    loads[4].wait()
    stores.append(pltpu.make_async_copy(gw, gw_o, sem.at[9]))
    stores[-1].start()
    for store in stores:
        store.wait()


def kernel(q_in, k_in, v_in, g_in, w_in, rows_o, gw_o, *scratch):
    s = dict(zip(NAMES, scratch[: len(NAMES)]))
    ssem, rsem, lsem = scratch[len(NAMES) :]
    dp = lax.axis_index("dp")
    me = lax.axis_index("seq")
    core = me % 2
    x_at = (me // 2) % 4
    z_at = me // 8

    def flipped(bits):
        out = me
        for bit in range(5):
            if bits >> bit & 1:
                out = out + (1 - 2 * ((me // 2**bit) % 2)) * 2**bit
        return out

    def flip2(at, k):
        out = at
        for bit in range(2):
            if k >> bit & 1:
                out = out + (1 - 2 * ((at // 2**bit) % 2)) * 2**bit
        return out

    peers = [(dp, flipped(b)) for b in (1, 2, 4, 6, 8, 16, 24)]
    peers += [(flip2(dp, k), me) for k in (1, 2, 3)]
    barrier = pltpu.get_barrier_semaphore()
    for peer in peers:
        pl.semaphore_signal(barrier, inc=1, device_id=peer, device_id_type=MESH)

    loads = []
    for i, src in enumerate((k_in, v_in, q_in, g_in)):
        loads.append(pltpu.make_async_copy(src, s["raw"].at[i], lsem.at[i]))
    loads.append(pltpu.make_async_copy(w_in, s["w"], lsem.at[4]))
    for load in loads:
        load.start()

    sent = []
    counter = [0]
    by_name = {}

    def send(name, src, dst, device):
        i = counter[0]
        counter[0] += 1
        copy = pltpu.make_async_remote_copy(
            src_ref=src,
            dst_ref=dst,
            send_sem=ssem.at[i],
            recv_sem=rsem.at[i],
            device_id=device,
            device_id_type=MESH,
        )
        copy.start()
        sent.append(copy)
        by_name[name] = copy

    def got(name):
        by_name[name].wait_recv()

    def to(bits):
        return (dp, flipped(bits))

    s["perm"][...] = reordering(0)

    def loop(n, f):
        for i in range(n):
            f(i)

    def at(i, width=HD):
        if isinstance(i, int):
            return pl.ds(i * width, width)
        return pl.ds(pl.multiple_of(i * width, width), width)

    def reorder(i):
        def chunk(c):
            s["tok"][i, :, at(c, 256)] = dot(s["perm"][...], s["raw"][i, :, at(c, 256)]).astype(BF16)

        loop(4, chunk)

    def halves(x):
        return (fold(x.astype(F32)) * 0.5).astype(BF16)

    loads[0].wait()
    reorder(0)
    loads[1].wait()
    reorder(1)

    def pyramid(c):
        fives = []
        for i in range(2):
            x = s["tok"][i, :, at(c, 256)]
            for level in range(1, 5):
                x = halves(x)
                s["own%d" % level][i, :, at(c, 256)] = x
            fives.append(fold(x.astype(F32)) * 0.5)
        s["own5"][:, at(c, 256)] = jnp.concatenate(fives, axis=0).astype(BF16)

    loop(4, pyramid)
    pl.semaphore_wait(barrier, len(peers))
    send("f5z3", s["own5"], s["land5"].at[0], to(Z3))
    send("f5z2", s["own5"], s["land5"].at[1], to(Z2))
    send("f4z1", s["own4"], s["sib4"].at[:, pl.ds(0, 16)], to(Z1))
    send("f3x3", s["own3"], s["sib3"].at[:, pl.ds(0, 32)], to(X3))
    send("f2x1", s["own2"], s["sib2"].at[:, pl.ds(0, 64)], to(X1))
    send("f1", s["own1"], s["sib1"], to(CORE))

    def relay(name, was, level, n, bits):
        got(was)
        if level == 5:
            g = n // 8
            send(name, s["land5"].at[pl.ds(0, g)], s["land5"].at[pl.ds(g, g)], to(bits))
        else:
            ref = s["sib%d" % level]
            send(name, ref.at[:, pl.ds(0, n)], ref.at[:, pl.ds(n, n)], to(bits))

    loads[2].wait()
    reorder(2)

    def q_pyramid(c):
        x = s["tok"][2, :, at(c, 256)]
        for level in range(1, 6):
            y = fold(x.astype(F32)) * 0.5
            x = y.astype(BF16)
            s["q%d" % level][:, at(c, 256)] = x

    loop(4, q_pyramid)
    loads[3].wait()
    reorder(3)
    relay("f4x1", "f4z1", 4, 16, X1)
    relay("f3x1", "f3x3", 3, 32, X1)
    loads[4].wait()

    def grad_att(c):
        s["ga"][:, at(c, 256)] = dot(s["tok"][3], s["w"][at(c, 256), :], 1, 1).astype(BF16)

    loop(4, grad_att)
    got("f5z2")
    relay("f5x1", "f5z3", 5, 16, X1)
    relay("f2c", "f2x1", 2, 64, CORE)
    relay("f4x3", "f4x1", 4, 32, X3)

    def zero_forward(h):
        sc = dot(s["tok"][2, :, at(h)], s["tok"][0, :, at(h)], 1, 1) * SCALE
        m = jnp.max(sc, axis=1, keepdims=True)
        e = jnp.exp(sc - m)
        s["d0"][h] = wide(jnp.sum(e, axis=1, keepdims=True))
        s["m0"][h] = wide(m)
        eb = e.astype(BF16)
        s["e0"][h] = eb
        s["n0"][h] = dot(eb, s["tok"][1, :, at(h)])

    loop(4, zero_forward)
    relay("f3c", "f3x1", 3, 64, CORE)
    relay("f5x3", "f5x1", 5, 32, X3)
    loop(4, lambda h: zero_forward(h + 4))
    relay("f4c", "f4x3", 4, 64, CORE)

    def groups(n):
        size = HEADS if n < 128 else 4
        return [range(h, h + size) for h in range(0, HEADS, size)]

    def coarse_forward(level):
        n = ROWS[level]
        sib = s["sib%d" % level]
        for heads in groups(n):
            part = [dot(s["q%d" % level][:, at(h)], sib[0, :, at(h)], 1, 1) for h in heads]
            sc = jnp.concatenate(part, axis=0) * SCALE + level * LOG_TWO
            m = jnp.max(sc, axis=1, keepdims=True)
            e = jnp.exp(sc - m)
            rows = pl.ds(heads[0] * n, len(heads) * n)
            s["e%d" % level][rows, :] = e
            s["m%d" % level][rows, :] = wide(m)
            s["d%d" % level][rows, :] = wide(jnp.sum(e, axis=1, keepdims=True))
            for i, h in enumerate(heads):
                eb = e[i * n : (i + 1) * n].astype(BF16)
                s["n%d" % level][at(h, n), :] = dot(eb, sib[1, :, at(h)])

    got("f1")
    coarse_forward(1)
    relay("f5c", "f5x3", 5, 64, CORE)
    got("f2c")
    coarse_forward(2)
    got("f3c")
    coarse_forward(3)
    got("f4c")
    coarse_forward(4)
    got("f5c")

    def unpack5(h):
        x = s["land5"][:, :, at(h)].astype(F32)
        s["sib5"][0, :, at(h)] = x[:, :8].reshape(128, HD).astype(BF16)
        s["sib5"][1, :, at(h)] = x[:, 8:].reshape(128, HD).astype(BF16)

    loop(HEADS, unpack5)
    coarse_forward(5)

    def merge(h):
        c, num, den = (s[name][at(h, 8), :] for name in ("m5", "n5", "d5"))
        a, b = {}, {}
        for level in (4, 3, 2, 1):
            m = s["m%d" % level][at(h, ROWS[level]), :]
            spread = twice(c)
            c = jnp.maximum(m, spread)
            a[level] = jnp.exp(m - c)
            b[level] = jnp.exp(spread - c)
            num = s["n%d" % level][at(h, ROWS[level]), :] * a[level] + twice(num) * b[level]
            den = s["d%d" % level][at(h, ROWS[level]), :] * a[level] + twice(den) * b[level]
        m = s["m0"][h]
        spread = twice(c)
        c = jnp.maximum(m, spread)
        a0 = jnp.exp(m - c)
        b0 = jnp.exp(spread - c)
        num = s["n0"][h] * a0 + twice(num) * b0
        den = s["d0"][h] * a0 + twice(den) * b0
        inv = 1.0 / den
        att = (num * inv).astype(BF16)
        s["att"][:, at(h)] = att
        ga = s["ga"][:, at(h)].astype(F32)
        delta = wide(jnp.sum(ga * att.astype(F32), axis=1, keepdims=True))
        s["gam"][h] = a0 * inv
        s["del"][h] = delta
        weight = b0 * inv
        grad = fold(weight * ga)
        diff = fold(weight * delta)
        for level in range(1, 6):
            if level < 5:
                s["g%d" % level][at(h, ROWS[level]), :] = grad * a[level]
                s["t%d" % level][at(h, ROWS[level]), :] = diff * a[level]
                grad = fold(grad * b[level])
                diff = fold(diff * b[level])
            else:
                s["g5"][at(h, 8), :] = grad
                s["t5"][at(h, 8), :] = diff

    loop(HEADS, merge)

    other = 1 - core

    def weight_other(h):
        cols = pl.ds(pl.multiple_of(other * 512, 512), 512)
        s["g0s"][at(h), :] = dot(s["att"][:, at(h)], s["tok"][3, :, cols], 0, 0).astype(BF16)

    loop(HEADS, weight_other)
    send("g0", s["g0s"], s["g0r"], to(CORE))

    def coarse_backward(level):
        n = ROWS[level]
        sib = s["sib%d" % level]

        def finish_head(h, e, ds, grad):
            s["dq%d" % level][:, at(h)] = dot(ds, sib[0, :, at(h)]) * SCALE
            dk = dot(ds, s["q%d" % level][:, at(h)], 0, 0) * SCALE
            dv = dot(e.astype(BF16), grad, 0, 0)
            if level == 1:
                s["bs1_0"][0, :, at(h)] = dk.astype(BF16)
                s["bs1_0"][1, :, at(h)] = dv.astype(BF16)
            elif level < 5:
                for i, x in enumerate((dk, dv)):
                    s["acc%d" % level][i, :, at(h)] = x[:64]
                    s["bs%d_0" % level][i, :, at(h)] = x[64:].astype(BF16)
            else:
                pair = jnp.concatenate([dk.reshape(16, 8, HD), dv.reshape(16, 8, HD)], axis=1)
                s["acc5"][:, :, at(h)] = pair[:8]
                s["bs5_0"][:, :, at(h)] = pair[8:].astype(BF16)

        for heads in groups(n):
            grads = [s["g%d" % level][at(h, n), :].astype(BF16) for h in heads]
            part = [dot(g, sib[1, :, at(h)], 1, 1) for g, h in zip(grads, heads)]
            rows = pl.ds(heads[0] * n, len(heads) * n)
            e = s["e%d" % level][rows, :]
            ds = e * (jnp.concatenate(part, axis=0) - s["t%d" % level][rows, :])
            for i, h in enumerate(heads):
                mine = slice(i * n, (i + 1) * n)
                finish_head(h, e[mine], ds[mine].astype(BF16), grads[i])
        send("b%d_0" % level, s["bs%d_0" % level], s["br%d_0" % level], to(CORE))

    def back_step(level, i):
        got("b%d_%d" % (level, i - 1))
        rounds = BACK[level]
        bits, n = rounds[i]
        if level == 5 and i == 3:
            for c in range(4):
                total = s["acc5"][:2, :, at(c, 256)] + s["br5_2"][:, :, at(c, 256)].astype(F32)
                s["bs5_3"][:, :, at(c, 256)] = total[:1].astype(BF16)
                s["bs5_4"][:, :, at(c, 256)] = total[1:].astype(BF16)
            send("b5_3", s["bs5_3"], s["br5_3"], to(Z3))
            send("b5_4", s["bs5_4"], s["br5_4"], to(Z2))
            return
        held = rounds[i - 1][1]
        acc, came, out = (s[x % level] for x in ("acc%d", "br%%d_%d" % (i - 1), "bs%%d_%d" % i))

        def chunk(c):
            if level == 5:
                total = acc[: held // 8, :, at(c, 256)] + came[:, :, at(c, 256)].astype(F32)
                keep = (held - n) // 8
                out[:, :, at(c, 256)] = total[keep:].astype(BF16)
                if keep:
                    acc[:keep, :, at(c, 256)] = total[:keep]
            else:
                keep = held - n
                for j in range(2):
                    total = acc[j, :held, at(c, 256)] + came[j, :, at(c, 256)].astype(F32)
                    out[j, :, at(c, 256)] = total[keep:].astype(BF16)
                    if keep:
                        acc[j, :keep, at(c, 256)] = total[:keep]

        loop(4, chunk)
        send("b%d_%d" % (level, i), out, s["br%d_%d" % (level, i)], to(bits))

    coarse_backward(2)

    def weight_own(h):
        cols = pl.ds(pl.multiple_of(core * 512, 512), 512)
        s["gown"][at(h), :] = dot(s["att"][:, at(h)], s["tok"][3, :, cols], 0, 0)

    loop(HEADS, weight_own)
    back_step(2, 1)
    got("g0")

    def weight_sum(j):
        x = s["gown"][at(j, 64), :] + s["g0r"][at(j, 64), :].astype(F32)
        s["gown"][at(j, 64), :] = x
        s["ga1s"][j // 4, at(j % 4, 64), :] = x[:, :256].astype(BF16)
        s["gb1s"][j // 4, j % 4] = x[:, 256:].astype(BF16)

    loop(16, weight_sum)
    y_dev = [(flip2(dp, k), me) for k in (1, 2, 3)]
    z_dev = [(dp, flipped(8 * k)) for k in (1, 2, 3)]
    x_dev = [(dp, flipped(2 * k)) for k in (1, 2, 3)]
    for k in (1, 2, 3):
        send("ga1_%d" % k, s["ga1s"].at[flip2(dp, k)], s["ga1r"].at[k - 1], y_dev[k - 1])
        send("gb1_%d" % k, s["gb1s"].at[:, flip2(z_at, k)], s["gb1r"].at[k - 1], z_dev[k - 1])

    coarse_backward(5)
    coarse_backward(4)
    back_step(5, 1)
    coarse_backward(3)
    back_step(4, 1)
    back_step(3, 1)
    coarse_backward(1)
    back_step(5, 2)
    back_step(4, 2)

    def zero_backward(h):
        e = s["e0"][h]
        q, ga = s["tok"][2, :, at(h)], s["ga"][:, at(h)]
        k, v = s["tok"][0, :, at(h)], s["tok"][1, :, at(h)]
        gam, delta = s["gam"][h], s["del"][h]
        both = jnp.concatenate([delta, delta], axis=1)
        ds = (e.astype(F32) * (dot(ga, v, 1, 1) - both)).astype(BF16)
        gq = (q.astype(F32) * gam).astype(BF16)
        gg = (ga.astype(F32) * gam).astype(BF16)
        s["kv0"][0, :, at(h)] = dot(ds, gq, 0, 0) * SCALE
        s["kv0"][1, :, at(h)] = dot(e, gg, 0, 0)
        up = s["dq5"][:, at(h)]
        for level in (4, 3, 2, 1):
            up = s["dq%d" % level][:, at(h)] + 0.5 * twice(up)
        dq = dot(ds, k) * gam * SCALE + 0.5 * twice(up)
        s["dq"][:, at(h)] = dq.astype(BF16)

    loop(4, zero_backward)
    back_step(3, 2)
    back_step(4, 3)
    back_step(5, 3)

    def weight_first():
        for k in (1, 2, 3):
            got("ga1_%d" % k)
            got("gb1_%d" % k)

        def chunk(j):
            r = pl.ds(pl.multiple_of(dp * 256 + j * 64, 64), 64)
            x = s["gown"][r, :256]
            for k in range(3):
                x = x + s["ga1r"][k, at(j, 64), :].astype(F32)
            s["ga2f"][j] = x
            s["ga2s"][j] = x.astype(BF16)
            r = pl.ds(pl.multiple_of(j * 256 + z_at * 64, 64), 64)
            x = s["gown"][r, 256:]
            for k in range(3):
                x = x + s["gb1r"][k, j].astype(F32)
            s["gb2f"][j] = x
            s["gb2s"][j] = x.astype(BF16)

        loop(4, chunk)
        for k in (1, 2, 3):
            send("ga2_%d" % k, s["ga2s"].at[flip2(z_at, k)], s["ga2r"].at[k - 1], z_dev[k - 1])
            send("gb2_%d" % k, s["gb2s"].at[flip2(dp, k)], s["gb2r"].at[k - 1], y_dev[k - 1])

    loop(2, lambda h: zero_backward(h + 4))
    weight_first()
    loop(2, lambda h: zero_backward(h + 6))

    stores = []

    def store(i, src):
        copy = pltpu.make_async_copy(src, rows_o.at[i], lsem.at[5 + i])
        copy.start()
        stores.append(copy)

    store(1, s["dq"])

    def weight_second():
        for k in (1, 2, 3):
            got("ga2_%d" % k)
            got("gb2_%d" % k)
        a = s["ga2f"][z_at]
        b = s["gb2f"][dp]
        for k in range(3):
            a = a + s["ga2r"][k].astype(F32)
            b = b + s["gb2r"][k].astype(F32)
        x = jnp.concatenate([a, b], axis=1).reshape(4, 16, 512)
        s["gc1f"][...] = x
        s["gc1s"][...] = x.astype(BF16)
        for k in (1, 2, 3):
            send("gc1_%d" % k, s["gc1s"].at[flip2(x_at, k)], s["gc1r"].at[k - 1], x_dev[k - 1])

    weight_second()

    def mix(c):
        s["mixed"][:, at(c, 256)] = dot(s["att"][...], s["w"][:, at(c, 256)]).astype(BF16)

    loop(4, mix)
    store(0, s["mixed"])

    for k in (1, 2, 3):
        got("gc1_%d" % k)
    x = s["gc1f"][x_at]
    for k in range(3):
        x = x + s["gc1r"][k].astype(F32)
    s["gds"][0] = x[:8]
    s["gds"][1] = x[8:]
    send("gd", s["gds"].at[other], s["gdr"], to(CORE))

    for level in range(1, 6):
        got("b%d_%d" % (level, len(BACK[level]) - 1))
    got("b5_3")

    def finish(h):
        for i in range(2):
            up = s["br5_3"][0, :, at(h)].astype(F32) + s["br5_4"][0, :, at(h)].astype(F32)
            up = up[8 * i : 8 * i + 8]
            for level in (4, 3, 2, 1):
                own = s["br%d_%d" % (level, len(BACK[level]) - 1)][i, :, at(h)]
                up = own.astype(F32) + 0.5 * twice(up)
            up = s["kv0"][i, :, at(h)] + 0.5 * twice(up)
            s["fin"][i, :, at(h)] = up.astype(BF16)

    loop(HEADS, finish)
    store(2, s["fin"].at[0])
    store(3, s["fin"].at[1])

    factor = 1.0 / math.sqrt(4 * 8192)
    got("gd")
    mine = s["gds"][core]
    s["gout"][:, pl.ds(pl.multiple_of(core * 512, 512), 512)] = mine * factor
    s["gout"][:, pl.ds(pl.multiple_of(other * 512, 512), 512)] = s["gdr"][...] * factor
    last = pltpu.make_async_copy(s["gout"], gw_o, lsem.at[9])
    last.start()
    for copy in sent:
        copy.wait_send()
    for copy in stores:
        copy.wait()
    last.wait()


def body(queries, keys, values, grad_out, w_out):
    weight = jax.ShapeDtypeStruct((8, D), F32)
    rows, gw = pl.pallas_call(
        kernel,
        out_shape=(jax.ShapeDtypeStruct((4, TOK, D), BF16), weight),
        in_specs=[pl.BlockSpec(memory_space=pl.ANY)] * 5,
        out_specs=[pl.BlockSpec(memory_space=pl.ANY)] * 2,
        scratch_shapes=[pltpu.VMEM(*SCRATCH[name]) for name in NAMES]
        + [
            pltpu.SemaphoreType.DMA((COPIES,)),
            pltpu.SemaphoreType.DMA((COPIES,)),
            pltpu.SemaphoreType.DMA((10,)),
        ],
        compiler_params=pltpu.CompilerParams(
            collective_id=0, has_side_effects=True, vmem_limit_bytes=60 * 1024 * 1024
        ),
    )(queries[0], keys[0], values[0], grad_out[0], w_out)
    outs = pl.pallas_call(
        restore,
        out_shape=(jax.ShapeDtypeStruct((TOK, D), BF16),) * 4 + (weight,),
        in_specs=[pl.BlockSpec(memory_space=pl.ANY)] * 2,
        out_specs=[pl.BlockSpec(memory_space=pl.ANY)] * 5,
        scratch_shapes=[
            pltpu.VMEM((4, TOK, D), BF16),
            pltpu.VMEM((4, TOK, D), BF16),
            pltpu.VMEM((8, D), F32),
            pltpu.SemaphoreType.DMA((10,)),
        ],
        compiler_params=pltpu.CompilerParams(vmem_limit_bytes=60 * 1024 * 1024),
    )(rows, gw)
    return tuple(out[None] for out in outs[:4]) + (outs[4],)


def solution(mesh):
    tokens = P("dp", "seq", None)
    return jax.shard_map(
        body,
        mesh=mesh,
        in_specs=(tokens, tokens, tokens, tokens, P()),
        out_specs=(tokens, tokens, tokens, tokens, P(("dp", "seq"), None)),
        check_vma=False,
    )
```
